128 devices in a mesh: band: 8 (over z, core), mem: 16 (over x, y).
Axes of the slice: x: 4, y: 4, z: 4, core: 2. Of those that a mesh axis runs over, the one named last changes fastest.
Arguments:
- prior_ensemble: bfloat16 [1024, 262144], P('mem', 'band'), may hold values from -6 to 6
- perturbed_measurements: bfloat16 [1024, 16384], P('mem', 'band'), may hold values from -6 to 6
- solved_residuals: bfloat16 [1024, 16384], P('mem', 'band'), may hold values from -6 to 6
- localisation_matrix: float32 [8, 128, 128], replicated, may hold values from 0 to 1
- piece_owner_device: int32 [2048], P('band'), may hold values from 0 to 15, as said below
- measurement_group_matrix: int32 [2048, 6], P('band'), may hold values from 0 to 127, as said below
- localisation_factors: int32 [2048, 6], P('band'), may hold values from 0 to 7
Outputs:
- analysis: bfloat16 [1024, 262144], P('mem', 'band')
- spread: float32 [4096, 128], P(('band', 'mem'))
The draws below stay inside these ranges and needn't reach their ends.
Inputs may be any that keep to these rules, and one draw needn't show every extreme that they name: `piece_owner_device`: within a band, no owner has more than 32 patches, and in every band one owner has exactly 32. `measurement_group_matrix`: patch p of band b = p // 256 has the centre block c = b * 16 + (p - b * 256) // 16 and uses only blocks c - 2 to c + 2.
All inputs are finite; a program needn't handle non-finite values.
Results may differ from the reference program's by a relative error of at most 0.0065.
Values may be sent and summed in bfloat16 or wider, within the bound.
A program may use at most 192 MiB of HBM per device.

```python
import jax
import jax.numpy as jnp
from jax import lax

ENSEMBLE_SIZE = 1024
PIECE_SPAN = 128
OBLK = 128
NBLK = 6
NTAPER = 8
RIM_BLOCKS = 2
PATCH_DEV = 16
CAP = 32
PIECES_PER_STRIP = 256
PATCHES = 2048
VECTOR_SPAN = 262144
OB_BAND = 16
NOBS_BLK = 128
NOBS = 16384
SLOTS = 4096
N_BAND = 8
N_MEM = 16


def draw_piece_owner_device(key, part):
    owner_count = PIECES_PER_STRIP // PATCH_DEV

    def one_band(band_key):
        key_heavy, key_pick, key_order = jax.random.split(band_key, 3)
        heavy = jax.random.randint(key_heavy, (), 0, owner_count)
        picked = jax.random.permutation(key_pick, (owner_count - 1) * CAP)[:PIECES_PER_STRIP - CAP]
        others = (picked // CAP).astype(jnp.int32)
        others = others + (others >= heavy).astype(jnp.int32)
        labels = jnp.concatenate([jnp.full((CAP,), heavy, jnp.int32), others])
        shuffle = jax.random.permutation(key_order, PIECES_PER_STRIP)
        return labels[shuffle].astype(jnp.int32)
    band_keys = jax.random.split(jax.random.fold_in(key, 11), PATCHES // PIECES_PER_STRIP)
    return jax.vmap(one_band)(band_keys).reshape(PATCHES)


def draw_measurement_group_matrix(key, part):
    patch = jnp.arange(PATCHES, dtype=jnp.int32)
    strip_position = patch // PIECES_PER_STRIP
    within = patch % PIECES_PER_STRIP
    centre = strip_position * OB_BAND + within * OB_BAND // PIECES_PER_STRIP
    offsets = jax.random.randint(jax.random.fold_in(key, 23), (PATCHES, NBLK), -RIM_BLOCKS, RIM_BLOCKS + 1)
    return jnp.clip(centre[:, None] + offsets, 0, NOBS_BLK - 1).astype(jnp.int32)


def touch_ends(drawn, own_key, smallest, high):
    extent = drawn.shape
    place = [jax.random.randint(jax.random.fold_in(own_key, axis), (), 0, extent[axis]) for axis in range(len(extent))]
    drawn = drawn.at[tuple(place)].set(smallest)
    longest = extent.index(max(extent))
    place[longest] = (place[longest] + 1) % extent[longest]
    return drawn.at[tuple(place)].set(high)


def shard_levels(rng, shape, cuts, least, largest):
    loudness, own = 1.0, jax.random.fold_in(rng, 6)
    for axis_at, blocks in cuts:
        draws = jnp.exp(jax.random.uniform(jax.random.fold_in(own, axis_at), (blocks,), jnp.float32, least / len(cuts), largest / len(cuts)))
        loudness = loudness * jnp.repeat(draws, shape[axis_at] // blocks).reshape([-1 if axis == axis_at else 1 for axis in range(len(shape))])
    return loudness


def bell_draw(key, dims, scale, reach, cuts=(), kind=jnp.bfloat16):
    array = scale * jax.random.normal(key, dims, jnp.float32)
    if cuts:
        array = array * shard_levels(key, dims, cuts, -0.22, 0.18)
    return jnp.clip(array, -reach, reach).astype(kind)


def setup_inputs(seed: int = 0) -> dict:
    seeds = jax.random.split(jax.random.key(seed), 8)
    return {
        "prior_ensemble": bell_draw(seeds[0], (ENSEMBLE_SIZE, VECTOR_SPAN), 1.0, 6.0, ((0, 16), (1, 8))),
        "perturbed_measurements": bell_draw(seeds[1], (ENSEMBLE_SIZE, NOBS), 1.0, 6.0, ((0, 16), (1, 8))),
        "solved_residuals": bell_draw(seeds[2], (ENSEMBLE_SIZE, NOBS), 1.0, 6.0, ((0, 16), (1, 8))),
        "localisation_matrix": jnp.clip(jax.random.uniform(seeds[3], (NTAPER, PIECE_SPAN, OBLK), jnp.float32, 0.0, 1.0), 0.0, 1.0),
        "piece_owner_device": draw_piece_owner_device(jax.random.fold_in(seeds[7], 71), 0),
        "measurement_group_matrix": draw_measurement_group_matrix(jax.random.fold_in(seeds[7], 71), 0),
        "localisation_factors": touch_ends(jax.random.randint(seeds[6], (PATCHES, NBLK), 0, NTAPER), jax.random.fold_in(seeds[6], 1), 0, NTAPER - 1).astype(jnp.int32),
    }


def reference(prior_ensemble, perturbed_measurements, solved_residuals, localisation_matrix, piece_owner_device, measurement_group_matrix, localisation_factors):
    prior_per_strip = prior_ensemble.reshape(ENSEMBLE_SIZE, N_BAND, PIECES_PER_STRIP, PIECE_SPAN)
    obs_float = perturbed_measurements.astype(jnp.float32)
    obs_centre = jnp.mean(obs_float, axis=0)
    obs_dev = (obs_float - obs_centre).astype(jnp.bfloat16).reshape(ENSEMBLE_SIZE, NOBS_BLK, OBLK)
    solved = solved_residuals.reshape(ENSEMBLE_SIZE, NOBS_BLK, OBLK)

    def one_band(strip_position):
        ensemble_vectors = lax.dynamic_index_in_dim(prior_per_strip, strip_position, 1, keepdims=False)
        block_rows = lax.dynamic_slice_in_dim(measurement_group_matrix, strip_position * PIECES_PER_STRIP, PIECES_PER_STRIP, 0)
        taper_rows = lax.dynamic_slice_in_dim(localisation_factors, strip_position * PIECES_PER_STRIP, PIECES_PER_STRIP, 0)
        members_float = ensemble_vectors.astype(jnp.float32)
        centre = jnp.mean(members_float, axis=0)
        state_dev = (members_float - centre).astype(jnp.bfloat16)
        increment = jnp.zeros((ENSEMBLE_SIZE, PIECES_PER_STRIP, PIECE_SPAN), jnp.float32)
        for block_id in range(NBLK):
            obs_piece = jnp.take(obs_dev, block_rows[:, block_id], axis=1)
            solved_piece = jnp.take(solved, block_rows[:, block_id], axis=1)
            covariance = jnp.einsum("mie,mio->ieo", state_dev.astype(jnp.float32), obs_piece.astype(jnp.float32)) / (ENSEMBLE_SIZE - 1)
            weights = jnp.take(localisation_matrix, taper_rows[:, block_id], axis=0)
            tapered = (weights * covariance).astype(jnp.bfloat16)
            increment = increment + jnp.einsum("ieo,mio->mie", tapered.astype(jnp.float32), solved_piece.astype(jnp.float32))
        updated = (members_float + increment).astype(jnp.bfloat16)
        updated_float = updated.astype(jnp.float32)
        upd_centre = jnp.mean(updated_float, axis=0)
        variance = jnp.mean((updated_float - upd_centre) ** 2, axis=0)
        return updated, variance

    updated, variance = lax.map(one_band, jnp.arange(N_BAND))
    analysis = jnp.transpose(updated, (1, 0, 2, 3)).reshape(ENSEMBLE_SIZE, VECTOR_SPAN)
    owners = piece_owner_device.reshape(N_BAND, PIECES_PER_STRIP)
    owner_hits = (owners[:, :, None] == jnp.arange(N_MEM, dtype=jnp.int32)[None, None, :]).astype(jnp.int32)
    before = jnp.cumsum(owner_hits, axis=1) - owner_hits
    slot_rank = jnp.sum(before * owner_hits, axis=2)
    band_base = (jnp.arange(N_BAND, dtype=jnp.int32) * (N_MEM * CAP))[:, None]
    slot_row = (band_base + owners * CAP + slot_rank).astype(jnp.int32)
    spread = jnp.zeros((SLOTS, PIECE_SPAN), jnp.float32).at[slot_row.reshape(-1)].set(variance.reshape(-1, PIECE_SPAN))
    return analysis, spread
```

```python
import functools

import jax
import jax.numpy as jnp
from jax import lax
from jax.experimental import pallas as pl
from jax.experimental.pallas import tpu as pltpu
from jax.sharding import PartitionSpec as P

RIM = 2
SPAN = 128
PAIR = 2 * SPAN
F32 = jnp.float32
BF16 = jnp.bfloat16


def pair_weights(rel, fac, table, w_ref, pair, blocks, nblk, scale):
    for half in range(2):
        base = (2 * pair + half) * nblk
        tiles = [table[fac[base + k]] for k in range(nblk)]
        for j in range(blocks):
            total = None
            for k in range(nblk):
                term = jnp.where(rel[base + k] == j, scale, 0.0) * tiles[k]
                total = term if total is None else total + term
            w_ref[pl.ds(j * SPAN, SPAN), pl.ds(half * SPAN, SPAN)] = total


def pair_update(x_ref, u_ref, var_ref, ydt, s_all, w_ref, xd, cov, gain, inc):
    members = x_ref.shape[0]
    step = 128
    rows = [pl.ds(r, step) for r in range(0, members, step)]
    total = jnp.zeros((1, PAIR), F32)
    for r in rows:
        total = total + jnp.sum(x_ref[r, :].astype(F32), axis=0, keepdims=True)
    mean = total / members
    for r in rows:
        xd[r, :] = (x_ref[r, :].astype(F32) - mean).astype(BF16)
    cov[...] = jnp.dot(ydt[...], xd[...], preferred_element_type=F32)
    for r in range(0, cov.shape[0], step):
        r = pl.ds(r, step)
        gain[r, :] = (w_ref[r, :] * cov[r, :]).astype(BF16)
    inc[...] = jnp.dot(s_all[...], gain[...], preferred_element_type=F32)
    total = jnp.zeros((1, PAIR), F32)
    for r in rows:
        new = (x_ref[r, :].astype(F32) + inc[r, :]).astype(BF16)
        u_ref[r, :] = new
        total = total + jnp.sum(new.astype(F32), axis=0, keepdims=True)
    mean = total / members
    total = jnp.zeros((1, PAIR), F32)
    for r in rows:
        off = u_ref[r, :].astype(F32) - mean
        total = total + jnp.sum(off * off, axis=0, keepdims=True)
    var_ref[...] = total / members


def prepare_obs(obs, ydt, s_all, blocks):
    members = obs[0].shape[1]
    for j in range(blocks):
        y = obs[j][0].astype(F32)
        dev = y - jnp.sum(y, axis=0, keepdims=True) / members
        ydt[pl.ds(j * SPAN, SPAN), :] = jnp.transpose(dev).astype(BF16)
        s_all[:, pl.ds(j * SPAN, SPAN)] = obs[j][1]


def update_kernel(nblk, rel, fac, table, x_ref, *refs):
    blocks = 2 * RIM + 1
    obs, (u_ref, var_ref, ydt, s_all, w_ref, xd, cov, gain, inc) = refs[:blocks], refs[blocks:]
    members = x_ref.shape[0]
    pair = pl.program_id(0)

    @pl.when(pair == 0)
    def _():
        prepare_obs(obs, ydt, s_all, blocks)

    pair_weights(rel, fac, table, w_ref, pair, blocks, nblk, 1.0 / (members - 1))
    pair_update(x_ref, u_ref, var_ref.at[0], ydt, s_all, w_ref, xd, cov, gain, inc)


def update(rel, fac, table, x, obs):
    members, width = x.shape
    blocks = 2 * RIM + 1
    nblk = rel.shape[1]
    whole = lambda *shape: pl.BlockSpec(shape, lambda i, *_: (0,) * len(shape))
    u, var = pl.pallas_call(
        functools.partial(update_kernel, nblk),
        out_shape=(
            jax.ShapeDtypeStruct(x.shape, BF16),
            jax.ShapeDtypeStruct((width // PAIR, 1, PAIR), F32),
        ),
        grid_spec=pltpu.PrefetchScalarGridSpec(
            num_scalar_prefetch=2,
            grid=(width // PAIR,),
            in_specs=[
                whole(*table.shape),
                pl.BlockSpec((members, PAIR), lambda i, *_: (0, i)),
                *[whole(2, members, SPAN)] * blocks,
            ],
            out_specs=(
                pl.BlockSpec((members, PAIR), lambda i, *_: (0, i)),
                pl.BlockSpec((1, 1, PAIR), lambda i, *_: (i, 0, 0)),
            ),
            scratch_shapes=[
                pltpu.VMEM((blocks * SPAN, members), BF16),
                pltpu.VMEM((members, blocks * SPAN), BF16),
                pltpu.VMEM((blocks * SPAN, PAIR), F32),
                pltpu.VMEM((members, PAIR), BF16),
                pltpu.VMEM((blocks * SPAN, PAIR), F32),
                pltpu.VMEM((blocks * SPAN, PAIR), BF16),
                pltpu.VMEM((members, PAIR), F32),
            ],
        ),
        compiler_params=pltpu.CompilerParams(vmem_limit_bytes=48 << 20),
    )(rel.reshape(-1), fac.reshape(-1), table, x, *obs)
    return u, var.reshape(-1, SPAN)


def per_device(prior, perturbed, solved, taper, owner, groups, factors):
    mems, bands = lax.axis_size("mem"), lax.axis_size("band")
    me, band = lax.axis_index("mem"), lax.axis_index("band")
    patches = owner.shape[0]
    per_worker = patches // mems
    capacity = 2 * per_worker
    table = jnp.transpose(taper, (0, 2, 1))
    start = me * per_worker
    centre = band * mems + me
    rel = lax.dynamic_slice_in_dim(groups, start, per_worker, 0) - centre + RIM
    fac = lax.dynamic_slice_in_dim(factors, start, per_worker, 0)

    obs = jnp.stack([perturbed, solved])
    own = lax.all_to_all(obs, "mem", split_axis=2, concat_axis=1, tiled=True)
    count = mems * bands
    near = {0: own}
    for d in (1, -1, 2, -2):
        near[d] = lax.ppermute(own, ("band", "mem"), [(i, (i - d) % count) for i in range(count)])
    x = lax.all_to_all(prior, "mem", split_axis=1, concat_axis=0, tiled=True)
    updated, variance = update(rel, fac, table, x, [near[d] for d in range(-RIM, RIM + 1)])
    analysis = lax.all_to_all(updated, "mem", split_axis=0, concat_axis=1, tiled=True)
    every = lax.all_to_all(jnp.tile(variance, (mems, 1)), "mem", split_axis=0, concat_axis=0, tiled=True)
    mine = (owner == me).astype(jnp.int32)
    rank = jnp.cumsum(mine) - mine
    slots = jnp.arange(capacity, dtype=jnp.int32)
    selector = ((rank[None, :] == slots[:, None]) & (mine[None, :] == 1)).astype(F32)
    spread = jnp.dot(selector, every, precision=lax.Precision.HIGHEST, preferred_element_type=F32)
    return analysis, spread


def solution(mesh):
    return jax.shard_map(
        per_device,
        mesh=mesh,
        in_specs=(
            P("mem", "band"),
            P("mem", "band"),
            P("mem", "band"),
            P(),
            P("band"),
            P("band", None),
            P("band", None),
        ),
        out_specs=(P("mem", "band"), P(("band", "mem"), None)),
        check_vma=False,
    )
```

```python
import functools

import jax
import jax.numpy as jnp
from jax import lax
from jax.experimental import pallas as pl
from jax.experimental.pallas import tpu as pltpu
from jax.sharding import PartitionSpec as P

RIM = 2
BLOCKS = 2 * RIM + 1
SPAN = 128
PAIR = 2 * SPAN
SIDE = 4
F32 = jnp.float32
BF16 = jnp.bfloat16
MESH = pl.DeviceIdType.MESH
HOPS = ((0, 1), (1, 0), (0, 3), (3, 0), (1, 1), (3, 3), (1, 3), (3, 1), (0, 2), (2, 0), (1, 2), (2, 1), (3, 2), (2, 3), (2, 2))


def pair_weights(rel, fac, table, w_ref, pair, nblk, scale):
    for half in range(2):
        base = (2 * pair + half) * nblk
        tiles = [table[fac[base + k]] for k in range(nblk)]
        for j in range(BLOCKS):
            total = None
            for k in range(nblk):
                term = jnp.where(rel[base + k] == j, scale, 0.0) * tiles[k]
                total = term if total is None else total + term
            w_ref[pl.ds(j * SPAN, SPAN), pl.ds(half * SPAN, SPAN)] = total


def pair_update(x_ref, u_ref, ydt, s_all, w_ref, xd, cov, gain, inc):
    members = x_ref.shape[0]
    step = 128
    rows = [pl.ds(r, step) for r in range(0, members, step)]
    total = jnp.zeros((1, PAIR), F32)
    for r in rows:
        total = total + jnp.sum(x_ref[r, :].astype(F32), axis=0, keepdims=True)
    mean = total / members
    for r in rows:
        xd[r, :] = (x_ref[r, :].astype(F32) - mean).astype(BF16)
    cov[...] = jnp.dot(ydt[...], xd[...], preferred_element_type=F32)
    for r in range(0, cov.shape[0], step):
        r = pl.ds(r, step)
        gain[r, :] = (w_ref[r, :] * cov[r, :]).astype(BF16)
    inc[...] = jnp.dot(s_all[...], gain[...], preferred_element_type=F32)
    total = jnp.zeros((1, PAIR), F32)
    for r in rows:
        new = (x_ref[r, :].astype(F32) + inc[r, :]).astype(BF16)
        u_ref[r, :] = new
        total = total + jnp.sum(new.astype(F32), axis=0, keepdims=True)
    mean = total / members
    total = jnp.zeros((1, PAIR), F32)
    for r in rows:
        off = u_ref[r, :].astype(F32) - mean
        total = total + jnp.sum(off * off, axis=0, keepdims=True)
    return total / members


def place(band, w):
    return w


def kernel(
    nblk, mems, bands,
    rel, fac, table, owner, prior, perturbed, solved,
    out, spread,
    xbuf, ubuf, obs, ydt, s_all, weights, xd, cov, gain, inc, var_mine, var_all,
    own_sem, own_send, near_recv, near_send, in_recv, in_send, out_recv, out_send, var_recv, var_send,
):
    band, me = lax.axis_index("band"), lax.axis_index("mem")
    x, y = me // SIDE, me % SIDE
    worker = place(band, me)
    members = xbuf.shape[1]
    local = prior.shape[0]
    pairs = xbuf.shape[0]
    width = pairs * PAIR
    peers = [((x + dx) % SIDE) * SIDE + (y + dy) % SIDE for dx, dy in HOPS]
    rows = pl.ds(pl.multiple_of(me * local, local), local)

    def chain(step):
        g = (band * mems + worker + step + bands * mems) % (bands * mems)
        return {"band": g // mems, "mem": place(g // mems, g % mems)}

    right, left = chain(1), chain(-1)

    barrier = pltpu.get_barrier_semaphore()
    for peer in peers:
        pl.semaphore_signal(barrier, inc=1, device_id={"mem": peer}, device_id_type=MESH)
    for peer in (left, right):
        pl.semaphore_signal(barrier, inc=1, device_id=peer, device_id_type=MESH)
    pl.semaphore_wait(barrier, len(peers) + 2)

    def columns(w, pair):
        return pl.ds(pl.multiple_of(w * width + pair * PAIR, PAIR), PAIR)

    def all_of(ref, sem):
        return pltpu.make_async_copy(ref, ref, sem)

    for i, source in enumerate((perturbed, solved)):
        pltpu.make_async_copy(
            source.at[:, pl.ds(pl.multiple_of(worker * SPAN, SPAN), SPAN)], obs.at[RIM, i, rows, :], own_sem
        ).start()
        for peer in peers:
            w = place(band, peer)
            pltpu.make_async_remote_copy(
                source.at[:, pl.ds(pl.multiple_of(w * SPAN, SPAN), SPAN)],
                obs.at[RIM, i, rows, :],
                own_send, own_sem, device_id={"mem": peer}, device_id_type=MESH,
            ).start()

    def send_prior(pair, carry):
        pltpu.make_async_copy(prior.at[:, columns(worker, pair)], xbuf.at[pair, rows, :], in_recv.at[pair]).start()
        for peer in peers:
            pltpu.make_async_remote_copy(
                prior.at[:, columns(place(band, peer), pair)], xbuf.at[pair, rows, :],
                in_send, in_recv.at[pair], device_id={"mem": peer}, device_id_type=MESH,
            ).start()
        return carry

    def make_weights(pair, carry):
        pair_weights(rel, fac, table, weights.at[pair], pair, nblk, 1.0 / (members - 1))
        return carry

    def near_copy(source, target, slot, i, peer):
        return pltpu.make_async_remote_copy(
            obs.at[source, i], obs.at[target, i],
            near_send.at[slot, i], near_recv.at[slot, i], device_id=peer, device_id_type=MESH,
        )

    lax.fori_loop(0, 2, send_prior, 0)
    lax.fori_loop(0, 2, make_weights, 0)
    all_of(obs.at[RIM], own_sem).wait()
    first = [(near_copy(2, 1, 0, i, right), near_copy(2, 3, 1, i, left)) for i in range(2)]
    second = [(near_copy(1, 0, 2, i, right), near_copy(3, 4, 3, i, left)) for i in range(2)]
    for pair_of in first:
        for copy in pair_of:
            copy.start()
    lax.fori_loop(2, 4, send_prior, 0)
    lax.fori_loop(2, 4, make_weights, 0)
    for pair_of, onward in zip(first, second):
        for copy, relay in zip(pair_of, onward):
            copy.wait_recv()
            relay.start()
    lax.fori_loop(4, pairs, send_prior, 0)
    lax.fori_loop(4, pairs, make_weights, 0)
    for pair_of in second:
        for copy in pair_of:
            copy.wait_recv()

    for j in range(BLOCKS):
        block = obs[j, 0].astype(F32)
        dev = block - jnp.sum(block, axis=0, keepdims=True) / members
        ydt[pl.ds(j * SPAN, SPAN), :] = jnp.transpose(dev).astype(BF16)
        s_all[:, pl.ds(j * SPAN, SPAN)] = obs[j, 1]

    def update(pair, carry):
        all_of(xbuf.at[pair], in_recv.at[pair]).wait()
        var = pair_update(xbuf.at[pair], ubuf.at[pair], ydt, s_all, weights.at[pair], xd, cov, gain, inc)
        var_mine[pl.ds(pair, 1), :] = var
        target = columns(worker, pair)
        pltpu.make_async_copy(ubuf.at[pair, rows, :], out.at[:, target], out_recv).start()
        for peer in peers:
            theirs = pl.ds(pl.multiple_of(peer * local, local), local)
            pltpu.make_async_remote_copy(
                ubuf.at[pair, theirs, :], out.at[:, target],
                out_send, out_recv, device_id={"mem": peer}, device_id_type=MESH,
            ).start()
        return carry

    lax.fori_loop(0, pairs, update, 0)

    pltpu.make_async_copy(var_mine, var_all.at[worker], var_recv).start()
    for peer in peers:
        pltpu.make_async_remote_copy(
            var_mine, var_all.at[worker], var_send, var_recv, device_id={"mem": peer}, device_id_type=MESH
        ).start()

    mine = jnp.where(owner[...] == me, 1.0, 0.0).astype(F32)
    even, odd = mine[0:1, :], mine[1:2, :]
    count = even.shape[1]
    before = (
        lax.broadcasted_iota(jnp.int32, (count, count), 0) < lax.broadcasted_iota(jnp.int32, (count, count), 1)
    )
    rank = jnp.dot(
        jnp.broadcast_to(even + odd, (8, count)).astype(BF16),
        jnp.where(before, 1.0, 0.0).astype(BF16),
        preferred_element_type=F32,
    )[0:1, :]
    slots = lax.broadcasted_iota(jnp.int32, (spread.shape[0], count), 0).astype(F32)
    all_of(var_all, var_recv).wait()
    total = None
    for half, (hit, order) in enumerate(((even, rank), (odd, rank + even))):
        selector = jnp.where(slots == order, 1.0, 0.0) * hit
        values = var_all[:, :, pl.ds(half * SPAN, SPAN)].reshape(count, SPAN)
        term = jnp.dot(selector, values, precision=lax.Precision.HIGHEST, preferred_element_type=F32)
        total = term if total is None else total + term
    spread[...] = total

    for pair_of in first + second:
        for copy in pair_of:
            copy.wait_send()
    part = xbuf.at[:, pl.ds(0, members - local), :]
    all_of(obs.at[RIM, :, pl.ds(0, members - local), :], own_send).wait()
    all_of(part, in_send).wait()
    all_of(var_all.at[pl.ds(0, mems - 1)], var_send).wait()
    all_of(part, out_send).wait()
    all_of(out, out_recv).wait()


def per_device(prior, perturbed, solved, taper, owner, groups, factors):
    mems, bands = lax.axis_size("mem"), lax.axis_size("band")
    me, band = lax.axis_index("mem"), lax.axis_index("band")
    local, span = prior.shape
    members = local * mems
    patches, nblk = groups.shape
    per_worker = patches // mems
    pairs = per_worker // 2
    capacity = 2 * per_worker
    worker = place(band, me)
    table = jnp.transpose(taper, (0, 2, 1))
    start = worker * per_worker
    rel = lax.dynamic_slice_in_dim(groups, start, per_worker, 0) - (band * mems + worker) + RIM
    fac = lax.dynamic_slice_in_dim(factors, start, per_worker, 0)
    vmem = pl.BlockSpec(memory_space=pltpu.VMEM)
    smem = pl.BlockSpec(memory_space=pltpu.SMEM)
    hbm = pl.BlockSpec(memory_space=OUT_SPACE)
    rim = BLOCKS * SPAN
    dma = pltpu.SemaphoreType.DMA
    return pl.pallas_call(
        functools.partial(kernel, nblk, mems, bands),
        out_shape=(
            jax.ShapeDtypeStruct(prior.shape, BF16),
            jax.ShapeDtypeStruct((capacity, SPAN), F32),
        ),
        in_specs=[smem, smem, vmem, vmem] + [pl.BlockSpec(memory_space=pltpu.HBM)] * 3,
        out_specs=(hbm, vmem),
        scratch_shapes=[
            pltpu.VMEM((pairs, members, PAIR), BF16),
            pltpu.VMEM((pairs, members, PAIR), BF16),
            pltpu.VMEM((BLOCKS, 2, members, SPAN), BF16),
            pltpu.VMEM((rim, members), BF16),
            pltpu.VMEM((members, rim), BF16),
            pltpu.VMEM((pairs, rim, PAIR), F32),
            pltpu.VMEM((members, PAIR), BF16),
            pltpu.VMEM((rim, PAIR), F32),
            pltpu.VMEM((rim, PAIR), BF16),
            pltpu.VMEM((members, PAIR), F32),
            pltpu.VMEM((pairs, PAIR), F32),
            pltpu.VMEM((mems, pairs, PAIR), F32),
            dma, dma, dma((4, 2)), dma((4, 2)), dma((pairs,)), dma, dma, dma, dma, dma,
        ],
        compiler_params=pltpu.CompilerParams(
            collective_id=0, has_side_effects=True, vmem_limit_bytes=60 << 20
        ),
    )(
        rel.reshape(-1), fac.reshape(-1), table,
        jnp.transpose(owner.reshape(patches // 2, 2)), prior, perturbed, solved,
    )


OUT_SPACE = pltpu.HBM


def solution(mesh):
    return jax.shard_map(
        per_device,
        mesh=mesh,
        in_specs=(
            P("mem", "band"),
            P("mem", "band"),
            P("mem", "band"),
            P(),
            P("band"),
            P("band", None),
            P("band", None),
        ),
        out_specs=(P("mem", "band"), P(("band", "mem"), None)),
        check_vma=False,
    )
```

```python
import functools

import jax
import jax.numpy as jnp
from jax import lax
from jax.experimental import pallas as pl
from jax.experimental.pallas import tpu as pltpu
from jax.sharding import PartitionSpec as P

RIM = 2
BLOCKS = 2 * RIM + 1
SPAN = 128
PAIR = 2 * SPAN
SIDE = 4
CHUNK = 128
F32 = jnp.float32
BF16 = jnp.bfloat16
MESH = pl.DeviceIdType.MESH
HOPS = ((0, 1), (1, 0), (0, 3), (3, 0), (1, 1), (3, 3), (1, 3), (3, 1), (0, 2), (2, 0), (1, 2), (2, 1), (3, 2), (2, 3), (2, 2))


def pair_weights(groups, factors, table, w_ref, patch, first, scale):
    nblk = groups.shape[0]
    for half in range(2):
        tiles = [table[factors[k, patch + half]] for k in range(nblk)]
        for j in range(BLOCKS):
            total = None
            for k in range(nblk):
                term = jnp.where(groups[k, patch + half] == first + j, scale, 0.0) * tiles[k]
                total = term if total is None else total + term
            w_ref[pl.ds(j * SPAN, SPAN), pl.ds(half * SPAN, SPAN)] = total


def pair_update(x_ref, u_ref, ydt, s_all, w_ref, xd, cov, gain, inc):
    members = x_ref.shape[0]
    step = 128
    rows = [pl.ds(r, step) for r in range(0, members, step)]
    total = jnp.zeros((1, PAIR), F32)
    for r in rows:
        total = total + jnp.sum(x_ref[r, :].astype(F32), axis=0, keepdims=True)
    mean = total / members
    for r in rows:
        xd[r, :] = (x_ref[r, :].astype(F32) - mean).astype(BF16)
    cov[...] = jnp.dot(ydt[...], xd[...], preferred_element_type=F32)
    for r in range(0, cov.shape[0], step):
        r = pl.ds(r, step)
        gain[r, :] = (w_ref[r, :] * cov[r, :]).astype(BF16)
    inc[...] = jnp.dot(s_all[...], gain[...], preferred_element_type=F32)
    total = jnp.zeros((1, PAIR), F32)
    for r in rows:
        new = (x_ref[r, :].astype(F32) + inc[r, :]).astype(BF16)
        u_ref[r, :] = new
        total = total + jnp.sum(new.astype(F32), axis=0, keepdims=True)
    mean = total / members
    total = jnp.zeros((1, PAIR), F32)
    for r in rows:
        off = u_ref[r, :].astype(F32) - mean
        total = total + jnp.sum(off * off, axis=0, keepdims=True)
    return total / members


def mem_of(band, w):
    row = w // SIDE
    along = (w % SIDE - row + SIDE) % SIDE
    odd = band % 2
    return (1 - odd) * (row * SIDE + along) + odd * (along * SIDE + row)


def worker_of(band, mem):
    x, y = mem // SIDE, mem % SIDE
    odd = band % 2
    return ((1 - odd) * x + odd * y) * SIDE + (x + y) % SIDE


def kernel(
    mems, bands,
    groups, factors, taper, owner, prior, perturbed, solved,
    out, spread,
    xbuf, ubuf, obs, table, ydt, s_all, weights, xd, cov, gain, inc, var_mine, var_all,
    own_sem, own_send, near_recv, near_send, in_recv, in_send, out_recv, out_send, var_recv, var_send,
):
    band, me = lax.axis_index("band"), lax.axis_index("mem")
    x, y = me // SIDE, me % SIDE
    worker = worker_of(band, me)
    members = xbuf.shape[1]
    local = prior.shape[0]
    pairs = xbuf.shape[0]
    width = pairs * PAIR
    peers = [((x + dx) % SIDE) * SIDE + (y + dy) % SIDE for dx, dy in HOPS]
    rows = pl.ds(pl.multiple_of(me * local, local), local)

    def chain(step):
        g = (band * mems + worker + step + bands * mems) % (bands * mems)
        return {"band": g // mems, "mem": mem_of(g // mems, g % mems)}

    right, left = chain(1), chain(-1)

    barrier = pltpu.get_barrier_semaphore()
    for peer in peers:
        pl.semaphore_signal(barrier, inc=1, device_id={"mem": peer}, device_id_type=MESH)
    for peer in (left, right):
        pl.semaphore_signal(barrier, inc=1, device_id=peer, device_id_type=MESH)
    pl.semaphore_wait(barrier, len(peers) + 2)

    def columns(w, pair):
        return pl.ds(pl.multiple_of(w * width + pair * PAIR, PAIR), PAIR)

    def all_of(ref, sem):
        return pltpu.make_async_copy(ref, ref, sem)

    for i, source in enumerate((perturbed, solved)):
        pltpu.make_async_copy(
            source.at[:, pl.ds(pl.multiple_of(worker * SPAN, SPAN), SPAN)], obs.at[RIM, i, rows, :], own_sem
        ).start()
        for peer in peers:
            w = worker_of(band, peer)
            pltpu.make_async_remote_copy(
                source.at[:, pl.ds(pl.multiple_of(w * SPAN, SPAN), SPAN)],
                obs.at[RIM, i, rows, :],
                own_send, own_sem, device_id={"mem": peer}, device_id_type=MESH,
            ).start()

    def send_prior(pair, carry):
        pltpu.make_async_copy(prior.at[:, columns(worker, pair)], xbuf.at[pair, rows, :], in_recv.at[pair]).start()
        for peer in peers:
            pltpu.make_async_remote_copy(
                prior.at[:, columns(worker_of(band, peer), pair)], xbuf.at[pair, rows, :],
                in_send, in_recv.at[pair], device_id={"mem": peer}, device_id_type=MESH,
            ).start()
        return carry

    def make_weights(pair, carry):
        pair_weights(
            groups, factors, table, weights.at[pair], 2 * (worker * pairs + pair),
            band * mems + worker - RIM, 1.0 / (members - 1),
        )
        return carry

    def near_copy(source, target, slot, c, peer):
        piece = pl.ds(pl.multiple_of((c % chunks) * CHUNK, CHUNK), CHUNK)
        return pltpu.make_async_remote_copy(
            obs.at[source, c // chunks, piece, :], obs.at[target, c // chunks, piece, :],
            near_send.at[slot, c], near_recv.at[slot, c], device_id=peer, device_id_type=MESH,
        )

    chunks = members // CHUNK
    steps = (
        lambda c: near_copy(2, 1, 0, c, right), lambda c: near_copy(2, 3, 1, c, left),
        lambda c: near_copy(1, 0, 2, c, right), lambda c: near_copy(3, 4, 3, c, left),
    )

    def near_first(c, carry):
        steps[0](c).start()
        steps[1](c).start()
        return carry

    def near_relay(c, carry):
        for side in range(2):
            steps[side](c).wait_recv()
            steps[2 + side](c).start()
        return carry

    def near_last(c, carry):
        steps[2](c).wait_recv()
        steps[3](c).wait_recv()
        return carry

    def near_sent(c, carry):
        for step in steps:
            step(c).wait_send()
        return carry

    lax.fori_loop(0, 2, send_prior, 0)
    for t in range(table.shape[0]):
        table[t] = jnp.transpose(taper[t])
    lax.fori_loop(0, 2, make_weights, 0)
    all_of(obs.at[RIM], own_sem).wait()
    lax.fori_loop(0, 2 * chunks, near_first, 0)
    lax.fori_loop(2, 4, send_prior, 0)
    lax.fori_loop(2, 4, make_weights, 0)
    lax.fori_loop(0, 2 * chunks, near_relay, 0)
    lax.fori_loop(4, pairs, send_prior, 0)
    lax.fori_loop(4, pairs, make_weights, 0)
    lax.fori_loop(0, 2 * chunks, near_last, 0)

    for j in range(BLOCKS):
        block = obs[j, 0].astype(F32)
        dev = block - jnp.sum(block, axis=0, keepdims=True) / members
        ydt[pl.ds(j * SPAN, SPAN), :] = jnp.transpose(dev).astype(BF16)
        s_all[:, pl.ds(j * SPAN, SPAN)] = obs[j, 1]

    def update(pair, carry):
        all_of(xbuf.at[pair], in_recv.at[pair]).wait()
        var = pair_update(xbuf.at[pair], ubuf.at[pair], ydt, s_all, weights.at[pair], xd, cov, gain, inc)
        for half in range(2):
            var_mine[pl.ds(2 * pair + half, 1), :] = var[:, half * SPAN:(half + 1) * SPAN]
        target = columns(worker, pair)
        pltpu.make_async_copy(ubuf.at[pair, rows, :], out.at[:, target], out_recv).start()
        for peer in peers:
            theirs = pl.ds(pl.multiple_of(peer * local, local), local)
            pltpu.make_async_remote_copy(
                ubuf.at[pair, theirs, :], out.at[:, target],
                out_send, out_recv, device_id={"mem": peer}, device_id_type=MESH,
            ).start()
        return carry

    lax.fori_loop(0, pairs, update, 0)

    pltpu.make_async_copy(var_mine, var_all.at[worker], var_recv).start()
    for peer in peers:
        pltpu.make_async_remote_copy(
            var_mine, var_all.at[worker], var_send, var_recv, device_id={"mem": peer}, device_id_type=MESH
        ).start()

    mine = jnp.where(owner[...] == me, 1.0, 0.0).astype(F32)
    count = mine.shape[1]
    before = (
        lax.broadcasted_iota(jnp.int32, (count, count), 0) < lax.broadcasted_iota(jnp.int32, (count, count), 1)
    )
    rank = jnp.dot(
        jnp.broadcast_to(mine, (8, count)).astype(BF16),
        jnp.where(before, 1.0, 0.0).astype(BF16),
        preferred_element_type=F32,
    )[0:1, :]
    slots = lax.broadcasted_iota(jnp.int32, (spread.shape[0], count), 0).astype(F32)
    selector = jnp.where(slots == rank, 1.0, 0.0) * mine
    all_of(var_all, var_recv).wait()
    spread[...] = jnp.dot(
        selector, var_all[...].reshape(count, SPAN), precision=lax.Precision.HIGHEST, preferred_element_type=F32
    )

    lax.fori_loop(0, 2 * chunks, near_sent, 0)
    part = xbuf.at[:, pl.ds(0, members - local), :]
    all_of(obs.at[RIM, :, pl.ds(0, members - local), :], own_send).wait()
    all_of(part, in_send).wait()
    all_of(var_all.at[pl.ds(0, mems - 1)], var_send).wait()
    all_of(part, out_send).wait()
    all_of(out, out_recv).wait()


def per_device(prior, perturbed, solved, taper, owner, groups, factors):
    mems, bands = lax.axis_size("mem"), lax.axis_size("band")
    local = prior.shape[0]
    members = local * mems
    patches = owner.shape[0]
    per_worker = patches // mems
    pairs = per_worker // 2
    capacity = 2 * per_worker
    vmem = pl.BlockSpec(memory_space=pltpu.VMEM)
    smem = pl.BlockSpec(memory_space=pltpu.SMEM)
    hbm = pl.BlockSpec(memory_space=OUT_SPACE)
    rim = BLOCKS * SPAN
    dma = pltpu.SemaphoreType.DMA
    return pl.pallas_call(
        functools.partial(kernel, mems, bands),
        out_shape=(
            jax.ShapeDtypeStruct(prior.shape, BF16),
            jax.ShapeDtypeStruct((capacity, SPAN), F32),
        ),
        in_specs=[smem, smem, vmem, vmem] + [pl.BlockSpec(memory_space=pltpu.HBM)] * 3,
        out_specs=(hbm, vmem),
        scratch_shapes=[
            pltpu.VMEM((pairs, members, PAIR), BF16),
            pltpu.VMEM((pairs, members, PAIR), BF16),
            pltpu.VMEM((BLOCKS, 2, members, SPAN), BF16),
            pltpu.VMEM(taper.shape, F32),
            pltpu.VMEM((rim, members), BF16),
            pltpu.VMEM((members, rim), BF16),
            pltpu.VMEM((pairs, rim, PAIR), F32),
            pltpu.VMEM((members, PAIR), BF16),
            pltpu.VMEM((rim, PAIR), F32),
            pltpu.VMEM((rim, PAIR), BF16),
            pltpu.VMEM((members, PAIR), F32),
            pltpu.VMEM((per_worker, SPAN), F32),
            pltpu.VMEM((mems, per_worker, SPAN), F32),
            dma, dma, dma((4, 2 * members // CHUNK)), dma((4, 2 * members // CHUNK)), dma((pairs,)), dma, dma, dma, dma, dma,
        ],
        compiler_params=pltpu.CompilerParams(
            collective_id=0, has_side_effects=True, vmem_limit_bytes=60 << 20
        ),
    )(
        jnp.transpose(groups), jnp.transpose(factors), taper, owner.reshape(1, patches), prior, perturbed, solved,
    )


OUT_SPACE = pltpu.HBM


def solution(mesh):
    return jax.shard_map(
        per_device,
        mesh=mesh,
        in_specs=(
            P("mem", "band"),
            P("mem", "band"),
            P("mem", "band"),
            P(),
            P("band"),
            P("band", None),
            P("band", None),
        ),
        out_specs=(P("mem", "band"), P(("band", "mem"), None)),
        check_vma=False,
    )
```

```python
import functools

import jax
import jax.numpy as jnp
from jax import lax
from jax.experimental import pallas as pl
from jax.experimental.pallas import tpu as pltpu
from jax.sharding import PartitionSpec as P

RIM = 2
BLOCKS = 2 * RIM + 1
SPAN = 128
PAIR = 2 * SPAN
SIDE = 4
CHUNK = 512
EARLY = 2
AHEAD = 6
F32 = jnp.float32
BF16 = jnp.bfloat16
MESH = pl.DeviceIdType.MESH
HOPS = ((0, 1), (1, 0), (0, 3), (3, 0), (1, 1), (3, 3), (1, 3), (3, 1), (0, 2), (2, 0), (1, 2), (2, 1), (3, 2), (2, 3), (2, 2))


def pair_weights(groups, factors, table, w_ref, patch, first, scale):
    nblk = groups.shape[0]
    for half in range(2):
        tiles = [table[factors[k, patch + half]] for k in range(nblk)]
        for j in range(BLOCKS):
            total = None
            for k in range(nblk):
                term = jnp.where(groups[k, patch + half] == first + j, scale, 0.0) * tiles[k]
                total = term if total is None else total + term
            w_ref[pl.ds(j * SPAN, SPAN), pl.ds(half * SPAN, SPAN)] = total


def pair_update(x_ref, u_ref, ydt, s_all, w_ref, xd, cov, gain, inc):
    members = x_ref.shape[0]
    step = 128
    rows = [pl.ds(r, step) for r in range(0, members, step)]
    total = jnp.zeros((1, PAIR), F32)
    for r in rows:
        total = total + jnp.sum(x_ref[r, :].astype(F32), axis=0, keepdims=True)
    mean = total / members
    for r in rows:
        xd[r, :] = (x_ref[r, :].astype(F32) - mean).astype(BF16)
    cov[...] = jnp.dot(ydt[...], xd[...], preferred_element_type=F32)
    for r in range(0, cov.shape[0], step):
        r = pl.ds(r, step)
        gain[r, :] = (w_ref[r, :] * cov[r, :]).astype(BF16)
    inc[...] = jnp.dot(s_all[...], gain[...], preferred_element_type=F32)
    total = jnp.zeros((1, PAIR), F32)
    for r in rows:
        new = (x_ref[r, :].astype(F32) + inc[r, :]).astype(BF16)
        u_ref[r, :] = new
        total = total + jnp.sum(new.astype(F32), axis=0, keepdims=True)
    mean = total / members
    total = jnp.zeros((1, PAIR), F32)
    for r in rows:
        off = u_ref[r, :].astype(F32) - mean
        total = total + jnp.sum(off * off, axis=0, keepdims=True)
    return total / members


def mem_of(band, w):
    row = w // SIDE
    along = (w % SIDE - row + SIDE) % SIDE
    odd = band % 2
    return (1 - odd) * (row * SIDE + along) + odd * (along * SIDE + row)


def worker_of(band, mem):
    x, y = mem // SIDE, mem % SIDE
    odd = band % 2
    return ((1 - odd) * x + odd * y) * SIDE + (x + y) % SIDE


def kernel(
    mems, bands,
    groups_hbm, factors_hbm, taper_hbm, owner_hbm, prior, perturbed, solved,
    out, spread,
    groups, factors, taper, owner, load_sem, xbuf, ubuf, obs, table, ydt, s_all, weights, xd, cov, gain, inc, var_mine, var_all,
    own_sem, own_send, near_recv, near_send, in_recv, in_send, out_recv, out_send, var_recv, var_send,
):
    band, me = lax.axis_index("band"), lax.axis_index("mem")
    x, y = me // SIDE, me % SIDE
    worker = worker_of(band, me)
    members = xbuf.shape[1]
    local = prior.shape[0]
    pairs = xbuf.shape[0]
    width = pairs * PAIR
    peers = [((x + dx) % SIDE) * SIDE + (y + dy) % SIDE for dx, dy in HOPS]
    rows = pl.ds(pl.multiple_of(me * local, local), local)

    def chain(step):
        g = (band * mems + worker + step + bands * mems) % (bands * mems)
        return {"band": g // mems, "mem": mem_of(g // mems, g % mems)}

    right, left = chain(1), chain(-1)

    barrier = pltpu.get_barrier_semaphore()
    for peer in reversed(peers):
        pl.semaphore_signal(barrier, inc=1, device_id={"mem": peer}, device_id_type=MESH)
    for peer in (left, right):
        pl.semaphore_signal(barrier, inc=1, device_id=peer, device_id_type=MESH)
    loads = [
        pltpu.make_async_copy(source, target, load_sem.at[i])
        for i, (source, target) in enumerate(
            ((taper_hbm, taper), (groups_hbm, groups), (factors_hbm, factors), (owner_hbm, owner))
        )
    ]
    for load in loads:
        load.start()

    def columns(w, pair):
        return pl.ds(pl.multiple_of(w * width + pair * PAIR, PAIR), PAIR)

    def all_of(ref, sem):
        return pltpu.make_async_copy(ref, ref, sem)

    def send_prior(pair, carry):
        pltpu.make_async_copy(prior.at[:, columns(worker, pair)], xbuf.at[pair, rows, :], in_recv.at[pair]).start()
        for peer in peers:
            pltpu.make_async_remote_copy(
                prior.at[:, columns(worker_of(band, peer), pair)], xbuf.at[pair, rows, :],
                in_send, in_recv.at[pair], device_id={"mem": peer}, device_id_type=MESH,
            ).start()
        return carry

    def make_weights(pair, carry):
        pair_weights(
            groups, factors, table, weights.at[pair], 2 * (worker * pairs + pair),
            band * mems + worker - RIM, 1.0 / (members - 1),
        )
        return carry

    def near_copy(source, target, slot, c, peer):
        piece = pl.ds(pl.multiple_of((c % chunks) * CHUNK, CHUNK), CHUNK)
        return pltpu.make_async_remote_copy(
            obs.at[source, c // chunks, piece, :], obs.at[target, c // chunks, piece, :],
            near_send.at[slot, c], near_recv.at[slot, c], device_id=peer, device_id_type=MESH,
        )

    chunks = members // CHUNK
    steps = (
        lambda c: near_copy(2, 1, 0, c, right), lambda c: near_copy(2, 3, 1, c, left),
        lambda c: near_copy(1, 0, 2, c, right), lambda c: near_copy(3, 4, 3, c, left),
    )

    def near_first(c, carry):
        steps[0](c).start()
        steps[1](c).start()
        return carry

    def near_relay(c, carry):
        for side in range(2):
            steps[side](c).wait_recv()
            steps[2 + side](c).start()
        return carry

    def near_last(c, carry):
        steps[2](c).wait_recv()
        steps[3](c).wait_recv()
        return carry

    def near_sent(c, carry):
        for step in steps:
            step(c).wait_send()
        return carry

    pl.semaphore_wait(barrier, len(peers) + 2)

    for i, source in enumerate((perturbed, solved)):
        pltpu.make_async_copy(
            source.at[:, pl.ds(pl.multiple_of(worker * SPAN, SPAN), SPAN)], obs.at[RIM, i, rows, :], own_sem
        ).start()
        for peer in peers:
            w = worker_of(band, peer)
            pltpu.make_async_remote_copy(
                source.at[:, pl.ds(pl.multiple_of(w * SPAN, SPAN), SPAN)],
                obs.at[RIM, i, rows, :],
                own_send, own_sem, device_id={"mem": peer}, device_id_type=MESH,
            ).start()

    lax.fori_loop(0, 2, send_prior, 0)
    for load in loads:
        load.wait()
    for t in range(table.shape[0]):
        table[t] = jnp.transpose(taper[t])
    lax.fori_loop(0, EARLY, make_weights, 0)
    all_of(obs.at[RIM], own_sem).wait()
    lax.fori_loop(0, 2 * chunks, near_first, 0)
    lax.fori_loop(2, 4, send_prior, 0)
    lax.fori_loop(0, 2 * chunks, near_relay, 0)
    lax.fori_loop(4, pairs, send_prior, 0)
    lax.fori_loop(EARLY, pairs, make_weights, 0)
    lax.fori_loop(0, 2 * chunks, near_last, 0)

    for j in range(BLOCKS):
        block = obs[j, 0].astype(F32)
        dev = block - jnp.sum(block, axis=0, keepdims=True) / members
        ydt[pl.ds(j * SPAN, SPAN), :] = jnp.transpose(dev).astype(BF16)
        s_all[:, pl.ds(j * SPAN, SPAN)] = obs[j, 1]

    def update(pair, carry):
        all_of(xbuf.at[pair], in_recv.at[pair]).wait()
        var = pair_update(xbuf.at[pair], ubuf.at[pair], ydt, s_all, weights.at[pair], xd, cov, gain, inc)
        for half in range(2):
            var_mine[pl.ds(2 * pair + half, 1), :] = var[:, half * SPAN:(half + 1) * SPAN]
        target = columns(worker, pair)

        def send_back(some):
            for peer in some:
                theirs = pl.ds(pl.multiple_of(peer * local, local), local)
                pltpu.make_async_remote_copy(
                    ubuf.at[pair, theirs, :], out.at[:, target],
                    out_send, out_recv, device_id={"mem": peer}, device_id_type=MESH,
                ).start()

        pltpu.make_async_copy(ubuf.at[pair, rows, :], out.at[:, target], out_recv).start()
        send_back(back[:AHEAD])

        @pl.when(pair == pairs - 1)
        def _():
            pltpu.make_async_copy(var_mine, var_all.at[worker], var_recv).start()
            for peer in back:
                pltpu.make_async_remote_copy(
                    var_mine, var_all.at[worker], var_send, var_recv, device_id={"mem": peer}, device_id_type=MESH
                ).start()

        send_back(back[AHEAD:])
        return carry

    back = peers[::-1]
    lax.fori_loop(0, pairs, update, 0)

    mine = jnp.where(owner[...] == me, 1.0, 0.0).astype(F32)
    count = mine.shape[1]
    before = (
        lax.broadcasted_iota(jnp.int32, (count, count), 0) < lax.broadcasted_iota(jnp.int32, (count, count), 1)
    )
    rank = jnp.dot(
        jnp.broadcast_to(mine, (8, count)).astype(BF16),
        jnp.where(before, 1.0, 0.0).astype(BF16),
        preferred_element_type=F32,
    )[0:1, :]
    slots = lax.broadcasted_iota(jnp.int32, (spread.shape[0], count), 0).astype(F32)
    selector = jnp.where(slots == rank, 1.0, 0.0) * mine
    all_of(var_all, var_recv).wait()
    spread[...] = jnp.dot(
        selector, var_all[...].reshape(count, SPAN), precision=lax.Precision.HIGHEST, preferred_element_type=F32
    )

    lax.fori_loop(0, 2 * chunks, near_sent, 0)
    part = xbuf.at[:, pl.ds(0, members - local), :]
    all_of(obs.at[RIM, :, pl.ds(0, members - local), :], own_send).wait()
    all_of(part, in_send).wait()
    all_of(var_all.at[pl.ds(0, mems - 1)], var_send).wait()
    all_of(part, out_send).wait()
    all_of(out, out_recv).wait()


def per_device(prior, perturbed, solved, taper, owner, groups, factors):
    mems, bands = lax.axis_size("mem"), lax.axis_size("band")
    local = prior.shape[0]
    members = local * mems
    patches = owner.shape[0]
    per_worker = patches // mems
    pairs = per_worker // 2
    capacity = 2 * per_worker
    hbm = pl.BlockSpec(memory_space=pltpu.HBM)
    rim = BLOCKS * SPAN
    dma = pltpu.SemaphoreType.DMA
    return pl.pallas_call(
        functools.partial(kernel, mems, bands),
        out_shape=(
            jax.ShapeDtypeStruct(prior.shape, BF16),
            jax.ShapeDtypeStruct((capacity, SPAN), F32),
        ),
        in_specs=[hbm] * 7,
        out_specs=(pl.BlockSpec(memory_space=OUT_SPACE), pl.BlockSpec(memory_space=pltpu.VMEM)),
        scratch_shapes=[
            pltpu.SMEM(groups.shape[::-1], jnp.int32),
            pltpu.SMEM(factors.shape[::-1], jnp.int32),
            pltpu.VMEM(taper.shape, F32),
            pltpu.VMEM((1, patches), jnp.int32),
            dma((4,)),
            pltpu.VMEM((pairs, members, PAIR), BF16),
            pltpu.VMEM((pairs, members, PAIR), BF16),
            pltpu.VMEM((BLOCKS, 2, members, SPAN), BF16),
            pltpu.VMEM(taper.shape, F32),
            pltpu.VMEM((rim, members), BF16),
            pltpu.VMEM((members, rim), BF16),
            pltpu.VMEM((pairs, rim, PAIR), F32),
            pltpu.VMEM((members, PAIR), BF16),
            pltpu.VMEM((rim, PAIR), F32),
            pltpu.VMEM((rim, PAIR), BF16),
            pltpu.VMEM((members, PAIR), F32),
            pltpu.VMEM((per_worker, SPAN), F32),
            pltpu.VMEM((mems, per_worker, SPAN), F32),
            dma, dma, dma((4, 2 * members // CHUNK)), dma((4, 2 * members // CHUNK)), dma((pairs,)), dma, dma, dma, dma, dma,
        ],
        compiler_params=pltpu.CompilerParams(
            collective_id=0, has_side_effects=True, vmem_limit_bytes=32 << 20
        ),
    )(
        *[pltpu.with_memory_space_constraint(a, pltpu.HBM) for a in (
            jnp.transpose(groups), jnp.transpose(factors), taper, owner.reshape(1, patches), prior, perturbed, solved
        )]
    )


OUT_SPACE = pltpu.HBM


def solution(mesh):
    return jax.shard_map(
        per_device,
        mesh=mesh,
        in_specs=(
            P("mem", "band"),
            P("mem", "band"),
            P("mem", "band"),
            P(),
            P("band"),
            P("band", None),
            P("band", None),
        ),
        out_specs=(P("mem", "band"), P(("band", "mem"), None)),
        check_vma=False,
    )
```

```python
import functools

import jax
import jax.numpy as jnp
from jax import lax
from jax.experimental import pallas as pl
from jax.experimental.pallas import tpu as pltpu
from jax.sharding import PartitionSpec as P

RIM = 2
BLOCKS = 2 * RIM + 1
SPAN = 128
PAIR = 2 * SPAN
SIDE = 4
CHUNK = 512
EARLY = 2
AHEAD = 6
PARTS = 8
F32 = jnp.float32
BF16 = jnp.bfloat16
MESH = pl.DeviceIdType.MESH
HOPS = ((0, 1), (1, 0), (0, 3), (3, 0), (1, 1), (3, 3), (1, 3), (3, 1), (0, 2), (2, 0), (1, 2), (2, 1), (3, 2), (2, 3), (2, 2))


def pair_weights(groups, factors, table, w_ref, patch, first, scale):
    nblk = groups.shape[0]
    for half in range(2):
        tiles = [table[factors[k, patch + half]] for k in range(nblk)]
        for j in range(BLOCKS):
            total = None
            for k in range(nblk):
                term = jnp.where(groups[k, patch + half] == first + j, scale, 0.0) * tiles[k]
                total = term if total is None else total + term
            w_ref[pl.ds(j * SPAN, SPAN), pl.ds(half * SPAN, SPAN)] = total


def pair_update(x_ref, u_ref, ydt, s_all, w_ref, xd, cov, gain, inc):
    members = x_ref.shape[0]
    step = 128
    rows = [pl.ds(r, step) for r in range(0, members, step)]
    total = jnp.zeros((1, PAIR), F32)
    for r in rows:
        total = total + jnp.sum(x_ref[r, :].astype(F32), axis=0, keepdims=True)
    mean = total / members
    for r in rows:
        xd[r, :] = (x_ref[r, :].astype(F32) - mean).astype(BF16)
    cov[...] = jnp.dot(ydt[...], xd[...], preferred_element_type=F32)
    for r in range(0, cov.shape[0], step):
        r = pl.ds(r, step)
        gain[r, :] = (w_ref[r, :] * cov[r, :]).astype(BF16)
    inc[...] = jnp.dot(s_all[...], gain[...], preferred_element_type=F32)
    total = jnp.zeros((1, PAIR), F32)
    for r in rows:
        new = (x_ref[r, :].astype(F32) + inc[r, :]).astype(BF16)
        u_ref[r, :] = new
        total = total + jnp.sum(new.astype(F32), axis=0, keepdims=True)
    mean = total / members
    total = jnp.zeros((1, PAIR), F32)
    for r in rows:
        off = u_ref[r, :].astype(F32) - mean
        total = total + jnp.sum(off * off, axis=0, keepdims=True)
    return total / members


def mem_of(band, w):
    row = w // SIDE
    along = (w % SIDE - row + SIDE) % SIDE
    odd = band % 2
    return (1 - odd) * (row * SIDE + along) + odd * (along * SIDE + row)


def worker_of(band, mem):
    x, y = mem // SIDE, mem % SIDE
    odd = band % 2
    return ((1 - odd) * x + odd * y) * SIDE + (x + y) % SIDE


def kernel(
    mems, bands,
    groups_hbm, factors_hbm, taper_hbm, owner_hbm, prior, perturbed, solved,
    out, spread,
    groups, factors, taper, owner, load_sem, xbuf, ubuf, obs, table, ydt, s_all, weights, xd, cov, gain, inc, var_mine, var_all,
    own_sem, own_send, near_recv, near_send, in_recv, in_send, out_recv, out_send, var_recv, var_send,
):
    band, me = lax.axis_index("band"), lax.axis_index("mem")
    x, y = me // SIDE, me % SIDE
    worker = worker_of(band, me)
    members = xbuf.shape[1]
    local = prior.shape[0]
    pairs = xbuf.shape[0]
    width = pairs * PAIR
    peers = [((x + dx) % SIDE) * SIDE + (y + dy) % SIDE for dx, dy in HOPS]
    rows = pl.ds(pl.multiple_of(me * local, local), local)

    def chain(step):
        g = (band * mems + worker + step + bands * mems) % (bands * mems)
        return {"band": g // mems, "mem": mem_of(g // mems, g % mems)}

    right, left = chain(1), chain(-1)

    barrier = pltpu.get_barrier_semaphore()
    for peer in reversed(peers):
        pl.semaphore_signal(barrier, inc=1, device_id={"mem": peer}, device_id_type=MESH)
    for peer in (left, right):
        pl.semaphore_signal(barrier, inc=1, device_id=peer, device_id_type=MESH)
    loads = [
        pltpu.make_async_copy(source, target, load_sem.at[i])
        for i, (source, target) in enumerate(
            ((taper_hbm, taper), (groups_hbm, groups), (factors_hbm, factors), (owner_hbm, owner))
        )
    ]
    for load in loads:
        load.start()

    def columns(w, pair):
        return pl.ds(pl.multiple_of(w * width + pair * PAIR, PAIR), PAIR)

    def all_of(ref, sem):
        return pltpu.make_async_copy(ref, ref, sem)

    def send_prior(pair, carry):
        pltpu.make_async_copy(prior.at[:, columns(worker, pair)], xbuf.at[pair, rows, :], in_recv.at[pair]).start()
        for peer in peers:
            pltpu.make_async_remote_copy(
                prior.at[:, columns(worker_of(band, peer), pair)], xbuf.at[pair, rows, :],
                in_send, in_recv.at[pair], device_id={"mem": peer}, device_id_type=MESH,
            ).start()
        return carry

    def make_weights(pair, carry):
        pair_weights(
            groups, factors, table, weights.at[pair], 2 * (worker * pairs + pair),
            band * mems + worker - RIM, 1.0 / (members - 1),
        )
        return carry

    def near_copy(source, target, slot, c, peer):
        piece = pl.ds(pl.multiple_of((c % chunks) * CHUNK, CHUNK), CHUNK)
        return pltpu.make_async_remote_copy(
            obs.at[source, c // chunks, piece, :], obs.at[target, c // chunks, piece, :],
            near_send.at[slot, c], near_recv.at[slot, c], device_id=peer, device_id_type=MESH,
        )

    chunks = members // CHUNK
    steps = (
        lambda c: near_copy(2, 1, 0, c, right), lambda c: near_copy(2, 3, 1, c, left),
        lambda c: near_copy(1, 0, 2, c, right), lambda c: near_copy(3, 4, 3, c, left),
    )

    def near_first(c, carry):
        steps[0](c).start()
        steps[1](c).start()
        return carry

    def near_relay(c, carry):
        for side in range(2):
            steps[side](c).wait_recv()
            steps[2 + side](c).start()
        return carry

    def near_last(c, carry):
        steps[2](c).wait_recv()
        steps[3](c).wait_recv()
        return carry

    def near_sent(c, carry):
        for step in steps:
            step(c).wait_send()
        return carry

    pl.semaphore_wait(barrier, len(peers) + 2)

    for i, source in enumerate((perturbed, solved)):
        pltpu.make_async_copy(
            source.at[:, pl.ds(pl.multiple_of(worker * SPAN, SPAN), SPAN)], obs.at[RIM, i, rows, :], own_sem
        ).start()
        for peer in peers:
            w = worker_of(band, peer)
            pltpu.make_async_remote_copy(
                source.at[:, pl.ds(pl.multiple_of(w * SPAN, SPAN), SPAN)],
                obs.at[RIM, i, rows, :],
                own_send, own_sem, device_id={"mem": peer}, device_id_type=MESH,
            ).start()

    lax.fori_loop(0, 2, send_prior, 0)
    for load in loads:
        load.wait()
    for t in range(table.shape[0]):
        table[t] = jnp.transpose(taper[t])
    lax.fori_loop(0, EARLY, make_weights, 0)
    all_of(obs.at[RIM], own_sem).wait()
    lax.fori_loop(0, 2 * chunks, near_first, 0)
    lax.fori_loop(2, 4, send_prior, 0)
    lax.fori_loop(0, 2 * chunks, near_relay, 0)
    lax.fori_loop(4, pairs, send_prior, 0)
    lax.fori_loop(EARLY, pairs, make_weights, 0)
    lax.fori_loop(0, 2 * chunks, near_last, 0)

    for j in range(BLOCKS):
        block = obs[j, 0].astype(F32)
        dev = block - jnp.sum(block, axis=0, keepdims=True) / members
        ydt[pl.ds(j * SPAN, SPAN), :] = jnp.transpose(dev).astype(BF16)
        s_all[:, pl.ds(j * SPAN, SPAN)] = obs[j, 1]

    def update(pair, carry):
        all_of(xbuf.at[pair], in_recv.at[pair]).wait()
        var = pair_update(xbuf.at[pair], ubuf.at[pair], ydt, s_all, weights.at[pair], xd, cov, gain, inc)
        for half in range(2):
            var_mine[pl.ds(2 * pair + half, 1), :] = var[:, half * SPAN:(half + 1) * SPAN]
        target = columns(worker, pair)

        def send_back(some):
            for peer in some:
                theirs = pl.ds(pl.multiple_of(peer * local, local), local)
                pltpu.make_async_remote_copy(
                    ubuf.at[pair, theirs, :], out.at[:, target],
                    out_send, out_recv, device_id={"mem": peer}, device_id_type=MESH,
                ).start()

        pltpu.make_async_copy(ubuf.at[pair, rows, :], out.at[:, target], out_recv).start()
        send_back(back[:AHEAD])

        @pl.when(pair == pairs - 1)
        def _():
            pltpu.make_async_copy(var_mine, var_all.at[worker], var_recv).start()
            for peer in back:
                pltpu.make_async_remote_copy(
                    var_mine, var_all.at[worker], var_send, var_recv, device_id={"mem": peer}, device_id_type=MESH
                ).start()

        send_back(back[AHEAD:])
        return carry

    back = peers[::-1]
    lax.fori_loop(0, pairs, update, 0)

    mine = jnp.where(owner[...] == me, 1.0, 0.0).astype(F32)
    count = mine.shape[1]
    before = (
        lax.broadcasted_iota(jnp.int32, (count, count), 0) < lax.broadcasted_iota(jnp.int32, (count, count), 1)
    )
    rank = jnp.dot(
        jnp.broadcast_to(mine, (8, count)).astype(BF16),
        jnp.where(before, 1.0, 0.0).astype(BF16),
        preferred_element_type=F32,
    )[0:1, :]
    slots = lax.broadcasted_iota(jnp.int32, (spread.shape[0], count), 0).astype(F32)
    selector = jnp.where(slots == rank, 1.0, 0.0) * mine
    all_of(var_all, var_recv).wait()
    spread[...] = jnp.dot(
        selector, var_all[...].reshape(count, SPAN), precision=lax.Precision.HIGHEST, preferred_element_type=F32
    )

    lax.fori_loop(0, 2 * chunks, near_sent, 0)
    part = xbuf.at[:, pl.ds(0, members - local), :]
    all_of(obs.at[RIM, :, pl.ds(0, members - local), :], own_send).wait()
    all_of(part, in_send).wait()
    all_of(var_all.at[pl.ds(0, mems - 1)], var_send).wait()
    all_of(part, out_send).wait()
    all_of(out, out_recv).wait()


def store(analysis, spread, analysis_out, spread_out, sems):
    rows = analysis.shape[0] // PARTS
    copies = [
        pltpu.make_async_copy(analysis.at[pl.ds(i * rows, rows), :], analysis_out.at[pl.ds(i * rows, rows), :], sems.at[i])
        for i in range(PARTS)
    ]
    copies.append(pltpu.make_async_copy(spread, spread_out, sems.at[PARTS]))
    for copy in copies:
        copy.start()
    for copy in copies:
        copy.wait()


def per_device(prior, perturbed, solved, taper, owner, groups, factors):
    mems, bands = lax.axis_size("mem"), lax.axis_size("band")
    local = prior.shape[0]
    members = local * mems
    patches = owner.shape[0]
    per_worker = patches // mems
    pairs = per_worker // 2
    capacity = 2 * per_worker
    hbm = pl.BlockSpec(memory_space=pltpu.HBM)
    rim = BLOCKS * SPAN
    dma = pltpu.SemaphoreType.DMA
    analysis, spread = pl.pallas_call(
        functools.partial(kernel, mems, bands),
        out_shape=(
            jax.ShapeDtypeStruct(prior.shape, BF16),
            jax.ShapeDtypeStruct((capacity, SPAN), F32),
        ),
        in_specs=[hbm] * 7,
        out_specs=(pl.BlockSpec(memory_space=OUT_SPACE), pl.BlockSpec(memory_space=pltpu.VMEM)),
        scratch_shapes=[
            pltpu.SMEM(groups.shape[::-1], jnp.int32),
            pltpu.SMEM(factors.shape[::-1], jnp.int32),
            pltpu.VMEM(taper.shape, F32),
            pltpu.VMEM((1, patches), jnp.int32),
            dma((4,)),
            pltpu.VMEM((pairs, members, PAIR), BF16),
            pltpu.VMEM((pairs, members, PAIR), BF16),
            pltpu.VMEM((BLOCKS, 2, members, SPAN), BF16),
            pltpu.VMEM(taper.shape, F32),
            pltpu.VMEM((rim, members), BF16),
            pltpu.VMEM((members, rim), BF16),
            pltpu.VMEM((pairs, rim, PAIR), F32),
            pltpu.VMEM((members, PAIR), BF16),
            pltpu.VMEM((rim, PAIR), F32),
            pltpu.VMEM((rim, PAIR), BF16),
            pltpu.VMEM((members, PAIR), F32),
            pltpu.VMEM((per_worker, SPAN), F32),
            pltpu.VMEM((mems, per_worker, SPAN), F32),
            dma, dma, dma((4, 2 * members // CHUNK)), dma((4, 2 * members // CHUNK)), dma((pairs,)), dma, dma, dma, dma, dma,
        ],
        compiler_params=pltpu.CompilerParams(
            collective_id=0, has_side_effects=True, vmem_limit_bytes=32 << 20
        ),
    )(
        *[pltpu.with_memory_space_constraint(a, pltpu.HBM) for a in (
            jnp.transpose(groups), jnp.transpose(factors), taper, owner.reshape(1, patches), prior, perturbed, solved
        )]
    )
    return pl.pallas_call(
        store,
        out_shape=(
            jax.ShapeDtypeStruct(analysis.shape, analysis.dtype),
            jax.ShapeDtypeStruct(spread.shape, spread.dtype),
        ),
        in_specs=[pl.BlockSpec(memory_space=pl.ANY)] * 2,
        out_specs=(hbm, hbm),
        scratch_shapes=[dma((PARTS + 1,))],
        compiler_params=pltpu.CompilerParams(vmem_limit_bytes=1 << 20),
    )(analysis, spread)


OUT_SPACE = pltpu.HBM


def solution(mesh):
    return jax.shard_map(
        per_device,
        mesh=mesh,
        in_specs=(
            P("mem", "band"),
            P("mem", "band"),
            P("mem", "band"),
            P(),
            P("band"),
            P("band", None),
            P("band", None),
        ),
        out_specs=(P("mem", "band"), P(("band", "mem"), None)),
        check_vma=False,
    )
```

```python
import functools

import jax
import jax.numpy as jnp
from jax import lax
from jax.experimental import pallas as pl
from jax.experimental.pallas import tpu as pltpu
from jax.sharding import PartitionSpec as P

RIM = 2
BLOCKS = 2 * RIM + 1
SPAN = 128
PAIR = 2 * SPAN
SIDE = 4
CHUNK = 512
EARLY = 2
AHEAD = 6
PARTS = 8
F32 = jnp.float32
BF16 = jnp.bfloat16
MESH = pl.DeviceIdType.MESH
HOPS = ((0, 1), (1, 0), (0, 3), (3, 0), (0, 2), (1, 1), (3, 3), (1, 3), (3, 1), (2, 0), (2, 1), (1, 2), (2, 3), (3, 2), (2, 2))


def pair_weights(groups, factors, table, w_ref, patch, first, scale):
    nblk = groups.shape[0]
    for half in range(2):
        tiles = [table[factors[k, patch + half]] for k in range(nblk)]
        for j in range(BLOCKS):
            total = None
            for k in range(nblk):
                term = jnp.where(groups[k, patch + half] == first + j, scale, 0.0) * tiles[k]
                total = term if total is None else total + term
            w_ref[pl.ds(j * SPAN, SPAN), pl.ds(half * SPAN, SPAN)] = total


def pair_update(x_ref, u_ref, ydt, s_all, w_ref, xd, cov, gain, inc):
    members = x_ref.shape[0]
    step = 128
    rows = [pl.ds(r, step) for r in range(0, members, step)]
    total = jnp.zeros((1, PAIR), F32)
    for r in rows:
        total = total + jnp.sum(x_ref[r, :].astype(F32), axis=0, keepdims=True)
    mean = total / members
    for r in rows:
        xd[r, :] = (x_ref[r, :].astype(F32) - mean).astype(BF16)
    cov[...] = jnp.dot(ydt[...], xd[...], preferred_element_type=F32)
    for r in range(0, cov.shape[0], step):
        r = pl.ds(r, step)
        gain[r, :] = (w_ref[r, :] * cov[r, :]).astype(BF16)
    inc[...] = jnp.dot(s_all[...], gain[...], preferred_element_type=F32)
    total = jnp.zeros((1, PAIR), F32)
    for r in rows:
        new = (x_ref[r, :].astype(F32) + inc[r, :]).astype(BF16)
        u_ref[r, :] = new
        total = total + jnp.sum(new.astype(F32), axis=0, keepdims=True)
    mean = total / members
    total = jnp.zeros((1, PAIR), F32)
    for r in rows:
        off = u_ref[r, :].astype(F32) - mean
        total = total + jnp.sum(off * off, axis=0, keepdims=True)
    return total / members


def mem_of(band, w):
    row = w // SIDE
    along = (w % SIDE - row + SIDE) % SIDE
    odd = band % 2
    return (1 - odd) * (row * SIDE + along) + odd * (along * SIDE + row)


def worker_of(band, mem):
    x, y = mem // SIDE, mem % SIDE
    odd = band % 2
    return ((1 - odd) * x + odd * y) * SIDE + (x + y) % SIDE


def kernel(
    mems, bands,
    groups_hbm, factors_hbm, taper_hbm, owner_hbm, prior, perturbed, solved,
    out, spread,
    groups, factors, taper, owner, load_sem, xbuf, ubuf, obs, table, ydt, s_all, weights, xd, cov, gain, inc, var_mine, var_all,
    own_sem, own_send, near_recv, near_send, in_recv, in_send, out_recv, out_send, var_recv, var_send,
):
    band, me = lax.axis_index("band"), lax.axis_index("mem")
    x, y = me // SIDE, me % SIDE
    worker = worker_of(band, me)
    members = xbuf.shape[1]
    local = prior.shape[0]
    pairs = xbuf.shape[0]
    width = pairs * PAIR
    peers = [((x + dx) % SIDE) * SIDE + (y + dy) % SIDE for dx, dy in HOPS]
    rows = pl.ds(pl.multiple_of(me * local, local), local)

    def chain(step):
        g = (band * mems + worker + step + bands * mems) % (bands * mems)
        return {"band": g // mems, "mem": mem_of(g // mems, g % mems)}

    right, left = chain(1), chain(-1)

    barrier = pltpu.get_barrier_semaphore()
    for peer in reversed(peers):
        pl.semaphore_signal(barrier, inc=1, device_id={"mem": peer}, device_id_type=MESH)
    for peer in (left, right):
        pl.semaphore_signal(barrier, inc=1, device_id=peer, device_id_type=MESH)
    loads = [
        pltpu.make_async_copy(source, target, load_sem.at[i])
        for i, (source, target) in enumerate(
            ((taper_hbm, taper), (groups_hbm, groups), (factors_hbm, factors), (owner_hbm, owner))
        )
    ]
    for load in loads:
        load.start()

    def columns(w, pair):
        return pl.ds(pl.multiple_of(w * width + pair * PAIR, PAIR), PAIR)

    def all_of(ref, sem):
        return pltpu.make_async_copy(ref, ref, sem)

    def send_prior(pair, carry):
        for peer in peers:
            pltpu.make_async_remote_copy(
                prior.at[:, columns(worker_of(band, peer), pair)], xbuf.at[pair, rows, :],
                in_send, in_recv.at[pair], device_id={"mem": peer}, device_id_type=MESH,
            ).start()
        pltpu.make_async_copy(prior.at[:, columns(worker, pair)], xbuf.at[pair, rows, :], in_recv.at[pair]).start()
        return carry

    def make_weights(pair, carry):
        pair_weights(
            groups, factors, table, weights.at[pair], 2 * (worker * pairs + pair),
            band * mems + worker - RIM, 1.0 / (members - 1),
        )
        return carry

    def near_copy(source, target, slot, c, peer):
        piece = pl.ds(pl.multiple_of((c % chunks) * CHUNK, CHUNK), CHUNK)
        return pltpu.make_async_remote_copy(
            obs.at[source, c // chunks, piece, :], obs.at[target, c // chunks, piece, :],
            near_send.at[slot, c], near_recv.at[slot, c], device_id=peer, device_id_type=MESH,
        )

    chunks = members // CHUNK
    steps = (
        lambda c: near_copy(2, 1, 0, c, right), lambda c: near_copy(2, 3, 1, c, left),
        lambda c: near_copy(1, 0, 2, c, right), lambda c: near_copy(3, 4, 3, c, left),
    )

    def near_first(c, carry):
        steps[0](c).start()
        steps[1](c).start()
        return carry

    def near_relay(c, carry):
        for side in range(2):
            steps[side](c).wait_recv()
            steps[2 + side](c).start()
        return carry

    def near_last(c, carry):
        steps[2](c).wait_recv()
        steps[3](c).wait_recv()
        return carry

    def near_sent(c, carry):
        for step in steps:
            step(c).wait_send()
        return carry

    pl.semaphore_wait(barrier, len(peers) + 2)

    for i, source in enumerate((perturbed, solved)):
        pltpu.make_async_copy(
            source.at[:, pl.ds(pl.multiple_of(worker * SPAN, SPAN), SPAN)], obs.at[RIM, i, rows, :], own_sem
        ).start()
        for peer in peers:
            w = worker_of(band, peer)
            pltpu.make_async_remote_copy(
                source.at[:, pl.ds(pl.multiple_of(w * SPAN, SPAN), SPAN)],
                obs.at[RIM, i, rows, :],
                own_send, own_sem, device_id={"mem": peer}, device_id_type=MESH,
            ).start()

    lax.fori_loop(0, 2, send_prior, 0)
    for load in loads:
        load.wait()
    for t in range(table.shape[0]):
        table[t] = jnp.transpose(taper[t])
    lax.fori_loop(0, EARLY, make_weights, 0)
    all_of(obs.at[RIM], own_sem).wait()
    lax.fori_loop(0, 2 * chunks, near_first, 0)
    lax.fori_loop(2, 4, send_prior, 0)
    lax.fori_loop(0, 2 * chunks, near_relay, 0)
    lax.fori_loop(4, pairs, send_prior, 0)
    lax.fori_loop(EARLY, pairs, make_weights, 0)
    lax.fori_loop(0, 2 * chunks, near_last, 0)

    for j in range(BLOCKS):
        block = obs[j, 0].astype(F32)
        dev = block - jnp.sum(block, axis=0, keepdims=True) / members
        ydt[pl.ds(j * SPAN, SPAN), :] = jnp.transpose(dev).astype(BF16)
        s_all[:, pl.ds(j * SPAN, SPAN)] = obs[j, 1]

    def update(pair, carry):
        all_of(xbuf.at[pair], in_recv.at[pair]).wait()
        var = pair_update(xbuf.at[pair], ubuf.at[pair], ydt, s_all, weights.at[pair], xd, cov, gain, inc)
        for half in range(2):
            var_mine[pl.ds(2 * pair + half, 1), :] = var[:, half * SPAN:(half + 1) * SPAN]
        target = columns(worker, pair)

        def send_back(some):
            for peer in some:
                theirs = pl.ds(pl.multiple_of(peer * local, local), local)
                pltpu.make_async_remote_copy(
                    ubuf.at[pair, theirs, :], out.at[:, target],
                    out_send, out_recv, device_id={"mem": peer}, device_id_type=MESH,
                ).start()

        send_back(back[:AHEAD])

        @pl.when(pair == pairs - 1)
        def _():
            pltpu.make_async_copy(var_mine, var_all.at[worker], var_recv).start()
            for peer in back:
                pltpu.make_async_remote_copy(
                    var_mine, var_all.at[worker], var_send, var_recv, device_id={"mem": peer}, device_id_type=MESH
                ).start()

        send_back(back[AHEAD:])
        pltpu.make_async_copy(ubuf.at[pair, rows, :], out.at[:, target], out_recv).start()
        return carry

    back = peers[::-1]
    lax.fori_loop(0, pairs, update, 0)

    mine = jnp.where(owner[...] == me, 1.0, 0.0).astype(F32)
    count = mine.shape[1]
    before = (
        lax.broadcasted_iota(jnp.int32, (count, count), 0) < lax.broadcasted_iota(jnp.int32, (count, count), 1)
    )
    rank = jnp.dot(
        jnp.broadcast_to(mine, (8, count)).astype(BF16),
        jnp.where(before, 1.0, 0.0).astype(BF16),
        preferred_element_type=F32,
    )[0:1, :]
    slots = lax.broadcasted_iota(jnp.int32, (spread.shape[0], count), 0).astype(F32)
    selector = jnp.where(slots == rank, 1.0, 0.0) * mine
    all_of(var_all, var_recv).wait()
    spread[...] = jnp.dot(
        selector, var_all[...].reshape(count, SPAN), precision=lax.Precision.HIGHEST, preferred_element_type=F32
    )

    lax.fori_loop(0, 2 * chunks, near_sent, 0)
    part = xbuf.at[:, pl.ds(0, members - local), :]
    all_of(obs.at[RIM, :, pl.ds(0, members - local), :], own_send).wait()
    all_of(part, in_send).wait()
    all_of(var_all.at[pl.ds(0, mems - 1)], var_send).wait()
    all_of(part, out_send).wait()
    all_of(out, out_recv).wait()


def store(analysis, spread, analysis_out, spread_out, sems):
    rows = analysis.shape[0] // PARTS
    copies = [
        pltpu.make_async_copy(analysis.at[pl.ds(i * rows, rows), :], analysis_out.at[pl.ds(i * rows, rows), :], sems.at[i])
        for i in range(PARTS)
    ]
    copies.append(pltpu.make_async_copy(spread, spread_out, sems.at[PARTS]))
    for copy in copies:
        copy.start()
    for copy in copies:
        copy.wait()


def per_device(prior, perturbed, solved, taper, owner, groups, factors):
    mems, bands = lax.axis_size("mem"), lax.axis_size("band")
    local = prior.shape[0]
    members = local * mems
    patches = owner.shape[0]
    per_worker = patches // mems
    pairs = per_worker // 2
    capacity = 2 * per_worker
    hbm = pl.BlockSpec(memory_space=pltpu.HBM)
    rim = BLOCKS * SPAN
    dma = pltpu.SemaphoreType.DMA
    analysis, spread = pl.pallas_call(
        functools.partial(kernel, mems, bands),
        out_shape=(
            jax.ShapeDtypeStruct(prior.shape, BF16),
            jax.ShapeDtypeStruct((capacity, SPAN), F32),
        ),
        in_specs=[hbm] * 7,
        out_specs=(pl.BlockSpec(memory_space=OUT_SPACE), pl.BlockSpec(memory_space=pltpu.VMEM)),
        scratch_shapes=[
            pltpu.SMEM(groups.shape[::-1], jnp.int32),
            pltpu.SMEM(factors.shape[::-1], jnp.int32),
            pltpu.VMEM(taper.shape, F32),
            pltpu.VMEM((1, patches), jnp.int32),
            dma((4,)),
            pltpu.VMEM((pairs, members, PAIR), BF16),
            pltpu.VMEM((pairs, members, PAIR), BF16),
            pltpu.VMEM((BLOCKS, 2, members, SPAN), BF16),
            pltpu.VMEM(taper.shape, F32),
            pltpu.VMEM((rim, members), BF16),
            pltpu.VMEM((members, rim), BF16),
            pltpu.VMEM((pairs, rim, PAIR), F32),
            pltpu.VMEM((members, PAIR), BF16),
            pltpu.VMEM((rim, PAIR), F32),
            pltpu.VMEM((rim, PAIR), BF16),
            pltpu.VMEM((members, PAIR), F32),
            pltpu.VMEM((per_worker, SPAN), F32),
            pltpu.VMEM((mems, per_worker, SPAN), F32),
            dma, dma, dma((4, 2 * members // CHUNK)), dma((4, 2 * members // CHUNK)), dma((pairs,)), dma, dma, dma, dma, dma,
        ],
        compiler_params=pltpu.CompilerParams(
            collective_id=0, has_side_effects=True, vmem_limit_bytes=32 << 20
        ),
    )(
        *[pltpu.with_memory_space_constraint(a, pltpu.HBM) for a in (
            jnp.transpose(groups), jnp.transpose(factors), taper, owner.reshape(1, patches), prior, perturbed, solved
        )]
    )
    return pl.pallas_call(
        store,
        out_shape=(
            jax.ShapeDtypeStruct(analysis.shape, analysis.dtype),
            jax.ShapeDtypeStruct(spread.shape, spread.dtype),
        ),
        in_specs=[pl.BlockSpec(memory_space=pl.ANY)] * 2,
        out_specs=(hbm, hbm),
        scratch_shapes=[dma((PARTS + 1,))],
        compiler_params=pltpu.CompilerParams(vmem_limit_bytes=1 << 20),
    )(analysis, spread)


OUT_SPACE = pltpu.HBM


def solution(mesh):
    return jax.shard_map(
        per_device,
        mesh=mesh,
        in_specs=(
            P("mem", "band"),
            P("mem", "band"),
            P("mem", "band"),
            P(),
            P("band"),
            P("band", None),
            P("band", None),
        ),
        out_specs=(P("mem", "band"), P(("band", "mem"), None)),
        check_vma=False,
    )
```

```python
import functools

import jax
import jax.numpy as jnp
from jax import lax
from jax.experimental import pallas as pl
from jax.experimental.pallas import tpu as pltpu
from jax.sharding import PartitionSpec as P

RIM = 2
BLOCKS = 2 * RIM + 1
SPAN = 128
PAIR = 2 * SPAN
SIDE = 4
CHUNK = 512
EARLY = 2
AHEAD = 6
PARTS = 8
F32 = jnp.float32
BF16 = jnp.bfloat16
MESH = pl.DeviceIdType.MESH
HOPS = ((0, 1), (1, 0), (0, 3), (3, 0), (0, 2), (1, 1), (3, 3), (1, 3), (3, 1), (2, 0), (2, 1), (1, 2), (2, 3), (3, 2), (2, 2))


def pair_weights(groups, factors, table, w_ref, patch, first, scale):
    nblk = groups.shape[0]
    for half in range(2):
        tiles = [table[factors[k, patch + half]] for k in range(nblk)]
        for j in range(BLOCKS):
            total = None
            for k in range(nblk):
                term = jnp.where(groups[k, patch + half] == first + j, scale, 0.0) * tiles[k]
                total = term if total is None else total + term
            w_ref[pl.ds(j * SPAN, SPAN), pl.ds(half * SPAN, SPAN)] = total


def pair_update(x_ref, u_ref, ydt, s_all, w_ref, xd, cov, gain, inc):
    members = x_ref.shape[0]
    step = 128
    rows = [pl.ds(r, step) for r in range(0, members, step)]
    total = jnp.zeros((1, PAIR), F32)
    for r in rows:
        total = total + jnp.sum(x_ref[r, :].astype(F32), axis=0, keepdims=True)
    mean = total / members
    for r in rows:
        xd[r, :] = (x_ref[r, :].astype(F32) - mean).astype(BF16)
    cov[...] = jnp.dot(ydt[...], xd[...], preferred_element_type=F32)
    for r in range(0, cov.shape[0], step):
        r = pl.ds(r, step)
        gain[r, :] = (w_ref[r, :] * cov[r, :]).astype(BF16)
    inc[...] = jnp.dot(s_all[...], gain[...], preferred_element_type=F32)
    total = jnp.zeros((1, PAIR), F32)
    for r in rows:
        new = (x_ref[r, :].astype(F32) + inc[r, :]).astype(BF16)
        u_ref[r, :] = new
        total = total + jnp.sum(new.astype(F32), axis=0, keepdims=True)
    mean = total / members
    total = jnp.zeros((1, PAIR), F32)
    for r in rows:
        off = u_ref[r, :].astype(F32) - mean
        total = total + jnp.sum(off * off, axis=0, keepdims=True)
    return total / members


def mem_of(band, w):
    row = w // SIDE
    along = (w % SIDE - row + SIDE) % SIDE
    odd = band % 2
    return (1 - odd) * (row * SIDE + along) + odd * (along * SIDE + row)


def worker_of(band, mem):
    x, y = mem // SIDE, mem % SIDE
    odd = band % 2
    return ((1 - odd) * x + odd * y) * SIDE + (x + y) % SIDE


def kernel(
    mems, bands,
    groups_hbm, factors_hbm, taper_hbm, owner_hbm, prior, perturbed, solved,
    out, spread,
    groups, factors, taper, owner, load_sem, var_f32, xbuf, ubuf, obs, table, ydt, s_all, weights, xd, cov, gain, inc, var_mine, var_all,
    own_sem, own_send, near_recv, near_send, in_recv, in_send, out_recv, out_send, var_recv, var_send,
):
    band, me = lax.axis_index("band"), lax.axis_index("mem")
    x, y = me // SIDE, me % SIDE
    worker = worker_of(band, me)
    members = xbuf.shape[1]
    local = prior.shape[0]
    pairs = xbuf.shape[0]
    width = pairs * PAIR
    peers = [((x + dx) % SIDE) * SIDE + (y + dy) % SIDE for dx, dy in HOPS]
    rows = pl.ds(pl.multiple_of(me * local, local), local)

    def chain(step):
        g = (band * mems + worker + step + bands * mems) % (bands * mems)
        return {"band": g // mems, "mem": mem_of(g // mems, g % mems)}

    right, left = chain(1), chain(-1)

    barrier = pltpu.get_barrier_semaphore()
    for peer in reversed(peers):
        pl.semaphore_signal(barrier, inc=1, device_id={"mem": peer}, device_id_type=MESH)
    for peer in (left, right):
        pl.semaphore_signal(barrier, inc=1, device_id=peer, device_id_type=MESH)
    loads = [
        pltpu.make_async_copy(source, target, load_sem.at[i])
        for i, (source, target) in enumerate(
            ((taper_hbm, taper), (groups_hbm, groups), (factors_hbm, factors), (owner_hbm, owner))
        )
    ]
    for load in loads:
        load.start()

    def columns(w, pair):
        return pl.ds(pl.multiple_of(w * width + pair * PAIR, PAIR), PAIR)

    def all_of(ref, sem):
        return pltpu.make_async_copy(ref, ref, sem)

    def send_prior(pair, carry):
        for peer in peers:
            pltpu.make_async_remote_copy(
                prior.at[:, columns(worker_of(band, peer), pair)], xbuf.at[pair, rows, :],
                in_send, in_recv.at[pair], device_id={"mem": peer}, device_id_type=MESH,
            ).start()
        pltpu.make_async_copy(prior.at[:, columns(worker, pair)], xbuf.at[pair, rows, :], in_recv.at[pair]).start()
        return carry

    def make_weights(pair, carry):
        pair_weights(
            groups, factors, table, weights.at[pair], 2 * (worker * pairs + pair),
            band * mems + worker - RIM, 1.0 / (members - 1),
        )
        return carry

    def near_copy(source, target, slot, c, peer):
        piece = pl.ds(pl.multiple_of((c % chunks) * CHUNK, CHUNK), CHUNK)
        return pltpu.make_async_remote_copy(
            obs.at[source, c // chunks, piece, :], obs.at[target, c // chunks, piece, :],
            near_send.at[slot, c], near_recv.at[slot, c], device_id=peer, device_id_type=MESH,
        )

    chunks = members // CHUNK
    steps = (
        lambda c: near_copy(2, 1, 0, c, right), lambda c: near_copy(2, 3, 1, c, left),
        lambda c: near_copy(1, 0, 2, c, right), lambda c: near_copy(3, 4, 3, c, left),
    )

    def near_first(c, carry):
        steps[0](c).start()
        steps[1](c).start()
        return carry

    def near_relay(c, carry):
        for side in range(2):
            steps[side](c).wait_recv()
            steps[2 + side](c).start()
        return carry

    def near_last(c, carry):
        steps[2](c).wait_recv()
        steps[3](c).wait_recv()
        return carry

    def near_sent(c, carry):
        for step in steps:
            step(c).wait_send()
        return carry

    pl.semaphore_wait(barrier, len(peers) + 2)

    for i, source in enumerate((perturbed, solved)):
        pltpu.make_async_copy(
            source.at[:, pl.ds(pl.multiple_of(worker * SPAN, SPAN), SPAN)], obs.at[RIM, i, rows, :], own_sem
        ).start()
        for peer in peers:
            w = worker_of(band, peer)
            pltpu.make_async_remote_copy(
                source.at[:, pl.ds(pl.multiple_of(w * SPAN, SPAN), SPAN)],
                obs.at[RIM, i, rows, :],
                own_send, own_sem, device_id={"mem": peer}, device_id_type=MESH,
            ).start()

    lax.fori_loop(0, 2, send_prior, 0)
    for load in loads:
        load.wait()
    for t in range(table.shape[0]):
        table[t] = jnp.transpose(taper[t])
    lax.fori_loop(0, EARLY, make_weights, 0)
    all_of(obs.at[RIM], own_sem).wait()
    lax.fori_loop(0, 2 * chunks, near_first, 0)
    lax.fori_loop(2, 4, send_prior, 0)
    lax.fori_loop(0, 2 * chunks, near_relay, 0)
    lax.fori_loop(4, pairs, send_prior, 0)
    lax.fori_loop(EARLY, pairs, make_weights, 0)
    lax.fori_loop(0, 2 * chunks, near_last, 0)

    for j in range(BLOCKS):
        block = obs[j, 0].astype(F32)
        dev = block - jnp.sum(block, axis=0, keepdims=True) / members
        ydt[pl.ds(j * SPAN, SPAN), :] = jnp.transpose(dev).astype(BF16)
        s_all[:, pl.ds(j * SPAN, SPAN)] = obs[j, 1]

    def update(pair, carry):
        all_of(xbuf.at[pair], in_recv.at[pair]).wait()
        var = pair_update(xbuf.at[pair], ubuf.at[pair], ydt, s_all, weights.at[pair], xd, cov, gain, inc)
        for half in range(2):
            var_f32[pl.ds(2 * pair + half, 1), :] = var[:, half * SPAN:(half + 1) * SPAN]

        @pl.when(pair == pairs - 1)
        def _():
            var_mine[...] = var_f32[...].astype(BF16)

        target = columns(worker, pair)

        def send_back(some):
            for peer in some:
                theirs = pl.ds(pl.multiple_of(peer * local, local), local)
                pltpu.make_async_remote_copy(
                    ubuf.at[pair, theirs, :], out.at[:, target],
                    out_send, out_recv, device_id={"mem": peer}, device_id_type=MESH,
                ).start()

        send_back(back[:AHEAD])

        @pl.when(pair == pairs - 1)
        def _():
            pltpu.make_async_copy(var_mine, var_all.at[worker], var_recv).start()
            for peer in back:
                pltpu.make_async_remote_copy(
                    var_mine, var_all.at[worker], var_send, var_recv, device_id={"mem": peer}, device_id_type=MESH
                ).start()

        send_back(back[AHEAD:])
        pltpu.make_async_copy(ubuf.at[pair, rows, :], out.at[:, target], out_recv).start()
        return carry

    back = peers[::-1]
    lax.fori_loop(0, pairs, update, 0)

    mine = jnp.where(owner[...] == me, 1.0, 0.0).astype(F32)
    count = mine.shape[1]
    before = (
        lax.broadcasted_iota(jnp.int32, (count, count), 0) < lax.broadcasted_iota(jnp.int32, (count, count), 1)
    )
    rank = jnp.dot(
        jnp.broadcast_to(mine, (8, count)).astype(BF16),
        jnp.where(before, 1.0, 0.0).astype(BF16),
        preferred_element_type=F32,
    )[0:1, :]
    slots = lax.broadcasted_iota(jnp.int32, (spread.shape[0], count), 0).astype(F32)
    selector = jnp.where(slots == rank, 1.0, 0.0) * mine
    all_of(var_all, var_recv).wait()
    spread[...] = jnp.dot(
        selector, var_all[...].astype(F32).reshape(count, SPAN), precision=lax.Precision.HIGHEST, preferred_element_type=F32
    )

    lax.fori_loop(0, 2 * chunks, near_sent, 0)
    part = xbuf.at[:, pl.ds(0, members - local), :]
    all_of(obs.at[RIM, :, pl.ds(0, members - local), :], own_send).wait()
    all_of(part, in_send).wait()
    all_of(var_all.at[pl.ds(0, mems - 1)], var_send).wait()
    all_of(part, out_send).wait()
    all_of(out, out_recv).wait()


def store(analysis, spread, analysis_out, spread_out, sems):
    rows = analysis.shape[0] // PARTS
    copies = [
        pltpu.make_async_copy(analysis.at[pl.ds(i * rows, rows), :], analysis_out.at[pl.ds(i * rows, rows), :], sems.at[i])
        for i in range(PARTS)
    ]
    copies.append(pltpu.make_async_copy(spread, spread_out, sems.at[PARTS]))
    for copy in copies:
        copy.start()
    for copy in copies:
        copy.wait()


def per_device(prior, perturbed, solved, taper, owner, groups, factors):
    mems, bands = lax.axis_size("mem"), lax.axis_size("band")
    local = prior.shape[0]
    members = local * mems
    patches = owner.shape[0]
    per_worker = patches // mems
    pairs = per_worker // 2
    capacity = 2 * per_worker
    hbm = pl.BlockSpec(memory_space=pltpu.HBM)
    rim = BLOCKS * SPAN
    dma = pltpu.SemaphoreType.DMA
    analysis, spread = pl.pallas_call(
        functools.partial(kernel, mems, bands),
        out_shape=(
            jax.ShapeDtypeStruct(prior.shape, BF16),
            jax.ShapeDtypeStruct((capacity, SPAN), F32),
        ),
        in_specs=[hbm] * 7,
        out_specs=(pl.BlockSpec(memory_space=OUT_SPACE), pl.BlockSpec(memory_space=pltpu.VMEM)),
        scratch_shapes=[
            pltpu.SMEM(groups.shape[::-1], jnp.int32),
            pltpu.SMEM(factors.shape[::-1], jnp.int32),
            pltpu.VMEM(taper.shape, F32),
            pltpu.VMEM((1, patches), jnp.int32),
            dma((4,)),
            pltpu.VMEM((per_worker, SPAN), F32),
            pltpu.VMEM((pairs, members, PAIR), BF16),
            pltpu.VMEM((pairs, members, PAIR), BF16),
            pltpu.VMEM((BLOCKS, 2, members, SPAN), BF16),
            pltpu.VMEM(taper.shape, F32),
            pltpu.VMEM((rim, members), BF16),
            pltpu.VMEM((members, rim), BF16),
            pltpu.VMEM((pairs, rim, PAIR), F32),
            pltpu.VMEM((members, PAIR), BF16),
            pltpu.VMEM((rim, PAIR), F32),
            pltpu.VMEM((rim, PAIR), BF16),
            pltpu.VMEM((members, PAIR), F32),
            pltpu.VMEM((per_worker, SPAN), BF16),
            pltpu.VMEM((mems, per_worker, SPAN), BF16),
            dma, dma, dma((4, 2 * members // CHUNK)), dma((4, 2 * members // CHUNK)), dma((pairs,)), dma, dma, dma, dma, dma,
        ],
        compiler_params=pltpu.CompilerParams(
            collective_id=0, has_side_effects=True, vmem_limit_bytes=32 << 20
        ),
    )(
        *[pltpu.with_memory_space_constraint(a, pltpu.HBM) for a in (
            jnp.transpose(groups), jnp.transpose(factors), taper, owner.reshape(1, patches), prior, perturbed, solved
        )]
    )
    return pl.pallas_call(
        store,
        out_shape=(
            jax.ShapeDtypeStruct(analysis.shape, analysis.dtype),
            jax.ShapeDtypeStruct(spread.shape, spread.dtype),
        ),
        in_specs=[pl.BlockSpec(memory_space=pl.ANY)] * 2,
        out_specs=(hbm, hbm),
        scratch_shapes=[dma((PARTS + 1,))],
        compiler_params=pltpu.CompilerParams(vmem_limit_bytes=1 << 20),
    )(analysis, spread)


OUT_SPACE = pltpu.HBM


def solution(mesh):
    return jax.shard_map(
        per_device,
        mesh=mesh,
        in_specs=(
            P("mem", "band"),
            P("mem", "band"),
            P("mem", "band"),
            P(),
            P("band"),
            P("band", None),
            P("band", None),
        ),
        out_specs=(P("mem", "band"), P(("band", "mem"), None)),
        check_vma=False,
    )
```
